256 devices in a mesh: prompt: 8 (over x, y_lo), tensor: 32 (over z, y_hi, core).
Axes of the slice: x: 4, y: 4 (y_hi: 2, y_lo: 2; y = y_hi * 2 + y_lo), z: 8, core: 2. Of those that a mesh axis runs over, the one named last changes fastest.
Arguments:
- tokens: bfloat16 [8, 128, 8192], P('prompt')
- gate_weight: bfloat16 [8192, 28672], P('prompt', 'tensor'), may hold values from -0.0625 to 0.0625
- up_weight: bfloat16 [8192, 28672], P('prompt', 'tensor'), may hold values from -0.0625 to 0.0625
- down_weight: bfloat16 [28672, 8192], P('tensor', 'prompt')
- norm_gain: float32 [8192], P('prompt'), may hold values from 0.1 to 1.9
- unembed: bfloat16 [8192, 86016], P('prompt', 'tensor'), may hold values from -0.5 to 0.5
- guidance: float32 [8], replicated, may hold values from -1.5 to 2.5
- logit_bias: float32 [128, 86016], P('prompt', 'tensor'), may hold values from -2 to 322
Outputs:
- log_probs: float32 [128, 86016], P('prompt', 'tensor')
The draws below stay inside these ranges and needn't reach their ends.
All inputs are finite; a program needn't handle non-finite values.
Results may differ from the reference program's by a relative error of at most 0.0025.
Values may be sent and summed in bfloat16 or wider, within the bound.
No kernel may reach another device: no remote copies, remote signals or barrier semaphores. Data moves between devices by JAX's collectives and lax.ppermute only.
A program may use at most 64 MiB of HBM per device.

```python
import jax
import jax.numpy as jnp
from jax import lax

D = 8192
FF = 28672
VOCAB = 86016
R = 128
VARIANTS = 8


def draw_tokens(key, part):
    keys = jax.random.split(key, 3)
    base = jax.random.normal(keys[0], (VARIANTS, R, D), jnp.float32)
    row_scale = 10.0 ** jax.random.uniform(keys[1], (VARIANTS, R, 1), jnp.float32)
    position = jnp.arange(D, dtype=jnp.float32).reshape(1, 1, D) / D
    column_scale = 10.0 ** (0.5 * position + 0.5 * jax.random.uniform(keys[2], (1, 1, D), jnp.float32))
    return (0.1 * base * row_scale * column_scale).astype(jnp.bfloat16)


def draw_down_weight(key, part):
    keys = jax.random.split(key, 2)
    base = jax.random.normal(keys[0], (FF, D), jnp.float32)
    position = jnp.arange(D, dtype=jnp.float32).reshape(1, D) / D
    column_scale = 10.0 ** (0.5 * position) * jax.random.uniform(keys[1], (1, D), jnp.float32, 0.5, 1.5)
    return (0.6 * base * column_scale / FF ** 0.5).astype(jnp.bfloat16)


def draw_logit_bias(key, part):
    keys = jax.random.split(key, 1)
    base = jax.random.uniform(keys[0], (R, VOCAB), jnp.float32, -2.0, 2.0)
    return base.astype(jnp.float32)


def steps_of(stream_key, extent, cuts, least, largest):
    def one(axis_at, blocks):
        steps = jax.random.uniform(jax.random.fold_in(jax.random.fold_in(stream_key, 6), axis_at), (blocks,), jnp.float32, least / len(cuts), largest / len(cuts))
        return jnp.repeat(jnp.exp(steps), extent[axis_at] // blocks).reshape((-1,) + (1,) * (len(extent) - axis_at - 1))

    gain = one(*cuts[0])
    for cut in cuts[1:]:
        gain = gain * one(*cut)
    return gain


def normal_values(key, shape, deviation, bound, cuts=(), held_as=jnp.bfloat16):
    result = jax.random.normal(key, shape, jnp.float32) * deviation
    if len(cuts) > 0:
        result = steps_of(key, shape, cuts, -0.22, 0.18) * result
    return jnp.clip(result, min=-bound, max=bound).astype(held_as)


def setup_inputs(seed: int = 0) -> dict:
    key_list = jax.random.split(jax.random.key(seed), 9)
    return {
        "tokens": draw_tokens(jax.random.fold_in(key_list[8], 71), 0),
        "gate_weight": normal_values(key_list[1], (D, FF), D ** -0.5, 0.0625, ((0, 8), (1, 32))),
        "up_weight": normal_values(key_list[2], (D, FF), D ** -0.5, 0.0625, ((0, 8), (1, 32))),
        "down_weight": draw_down_weight(jax.random.fold_in(key_list[8], 71), 0),
        "norm_gain": jnp.clip(1.0 + 0.18 * jax.random.normal(key_list[4], (D,), jnp.float32), 0.1, 1.9),
        "unembed": normal_values(key_list[5], (D, VOCAB), (3.0 / D ** 0.5), 0.5, ((0, 8), (1, 32))),
        "guidance": jnp.clip(jax.random.uniform(key_list[6], (VARIANTS,), jnp.float32, -1.5, 2.5), -1.5, 2.5),
        "logit_bias": draw_logit_bias(jax.random.fold_in(key_list[8], 71), 0),
    }


def reference(tokens, gate_weight, up_weight, down_weight, norm_gain, unembed, guidance, logit_bias):
    flat = tokens.reshape(VARIANTS * R, D)
    gate = jnp.dot(flat, gate_weight, preferred_element_type=jnp.float32)
    up = jnp.dot(flat, up_weight, preferred_element_type=jnp.float32)
    hidden = (jax.nn.silu(gate) * up).astype(jnp.bfloat16)
    branch = jnp.dot(hidden, down_weight, preferred_element_type=jnp.float32)
    state = flat.astype(jnp.float32) + branch
    mean_square = lax.optimization_barrier(jnp.mean(state * state, axis=1, keepdims=True))
    normed = (state * lax.rsqrt(mean_square + 1e-05) * norm_gain).astype(jnp.bfloat16)
    guided = jnp.zeros((R, VOCAB), jnp.float32)
    for variant in range(VARIANTS):
        rows_now = normed[variant * R:(variant + 1) * R]
        guided = guided + guidance[variant] * jnp.dot(rows_now, unembed, preferred_element_type=jnp.float32)
    scores = guided + logit_bias
    return jax.nn.log_softmax(scores, axis=1)
```

```python
import jax
import jax.numpy as jnp
from jax import lax
from jax.sharding import Mesh
from jax.sharding import PartitionSpec as P

D = 8192
EPS = 1e-05
NX, NY, NZ, NW, NC = 4, 2, 8, 2, 2
AXES = ("x", "y", "z", "w", "c")
PROMPT = ("x", "y")
TENSOR = ("z", "w", "c")
BF, F32 = jnp.bfloat16, jnp.float32


def shifted(array, axis, size, step):
    return lax.ppermute(array, axis, [(i, (i + step) % size) for i in range(size)])


def from_prompt(array, dx, dy):
    pairs = [
        (((x + dx) % NX) * NY + (y ^ dy), x * NY + y) for x in range(NX) for y in range(NY)
    ]
    return lax.ppermute(array, PROMPT, pairs)


def wide(array):
    return array.astype(F32)


def tokens_for_block(tokens, x, y, c):
    half = tokens.shape[0] // NC
    share = D // (NX * NY)
    mine = lax.dynamic_slice_in_dim(tokens, c * half, half, 0)
    blocks = mine.reshape(half, NX * NY, share).transpose(1, 0, 2)
    own, other = [None] * NX, [None] * NX
    for d in (2, 1, 3, 0):
        parts = []
        for dy in range(NY):
            block = ((x - d) % NX) * NY + (y ^ dy)
            piece = lax.dynamic_index_in_dim(blocks, block, 0, keepdims=False)
            parts.append(piece if d == 0 and dy == 0 else from_prompt(piece, d, dy))
        own[d] = jnp.stack(parts)
    own = jnp.stack(own)
    other = shifted(own, "c", NC, 1)
    return own, other


def products(rows, weights):
    flat = rows.reshape(-1, rows.shape[-1])
    outs = [jnp.dot(flat, weight, preferred_element_type=F32) for weight in weights]
    return [out.reshape(*rows.shape[:-1], -1) for out in outs]


def joined(pair):
    return jnp.stack([part.astype(BF) for part in pair])


def local(tokens, gate_weight, up_weight, down_weight, norm_gain, unembed, guidance, logit_bias):
    x, y, z, w, c = (lax.axis_index(axis) for axis in AXES)
    tokens = tokens[0]
    own, other = tokens_for_block(tokens, x, y, c)
    both = (gate_weight, up_weight)

    gb, ub = products(other, both)
    ga, ua = products(own, both)
    swap_a = shifted(joined((ga[:, 1], ua[:, 1])), "y", NY, 1)
    got_b = [shifted(joined((gb[d], ub[d])), "x", NX, d) for d in (1, 3, 2)]
    sum_ga, sum_ua = ga[:, 0] + wide(swap_a[0]), ua[:, 0] + wide(swap_a[1])
    got_a = [shifted(joined((sum_ga[d], sum_ua[d])), "x", NX, d) for d in (1, 3, 2)]
    sum_gb = gb[0] + sum(wide(got[0]) for got in got_b)
    sum_ub = ub[0] + sum(wide(got[1]) for got in got_b)
    swap_b = shifted(joined((sum_gb[1], sum_ub[1])), "y", NY, 1)
    gate_b, up_b = sum_gb[0] + wide(swap_b[0]), sum_ub[0] + wide(swap_b[1])
    hidden_b = (jax.nn.silu(gate_b) * up_b).astype(BF)
    gate_a = sum_ga[0] + sum(wide(got[0]) for got in got_a)
    up_a = sum_ua[0] + sum(wide(got[1]) for got in got_a)
    hidden_a = (jax.nn.silu(gate_a) * up_a).astype(BF)

    line_b = [None] * NX
    line_b[0] = hidden_b
    for d in (1, 3, 2):
        line_b[d] = shifted(hidden_b, "x", NX, -d)
    line_b = jnp.stack(line_b)
    all_b = jnp.stack([line_b, shifted(line_b, "y", NY, 1)], axis=1)
    pair_a = jnp.stack([hidden_a, shifted(hidden_a, "y", NY, 1)])
    all_a = [None] * NX
    all_a[0] = pair_a
    for d in (1, 3, 2):
        all_a[d] = shifted(pair_a, "x", NX, -d)
    all_a = jnp.stack(all_a)

    (down_b,) = products(all_b, (down_weight,))
    passed = shifted(down_b.astype(BF), "c", NC, 1)
    (down_a,) = products(all_a, (down_weight,))
    share = down_a.shape[-1]
    part = down_a + wide(passed)
    part = part.reshape(NX * NY, NZ, -1, share)

    def piece(k):
        return lax.dynamic_index_in_dim(part, (z + k) % NZ, 1, keepdims=False)

    cut = NX * NY // 2
    far = piece(4).astype(BF)
    up_way = shifted(far[:cut], "z", NZ, 1)
    down_way = shifted(far[cut:], "z", NZ, -1)
    near, back = piece(3), piece(5)
    up_way = jnp.concatenate([near[:cut] + wide(up_way), near[cut:]]).astype(BF)
    down_way = jnp.concatenate([back[:cut], back[cut:] + wide(down_way)]).astype(BF)
    for k in (2, 1):
        up_way = (piece(k) + wide(shifted(up_way, "z", NZ, 1))).astype(BF)
        down_way = (piece(NZ - k) + wide(shifted(down_way, "z", NZ, -1))).astype(BF)
    up_way = shifted(up_way, "z", NZ, 1)
    down_way = shifted(down_way, "z", NZ, -1)
    mine = (piece(0) + wide(up_way) + wide(down_way)).astype(BF)
    branch = wide(mine) + wide(shifted(mine, "w", NW, 1))

    residual = own.reshape(NX * NY, NZ, -1, share)
    residual = lax.dynamic_index_in_dim(residual, z, 1, keepdims=False)
    state = wide(residual) + branch
    partial_square = jnp.sum(state * state, axis=2)
    offsets = jnp.arange(NX * NY)
    variant_at = ((x + offsets // NY) % NX) * NY + ((offsets % NY) ^ y)
    placed_at = (variant_at[None, :] == offsets[:, None]).astype(F32)
    by_variant = jnp.sum(placed_at[:, :, None] * partial_square[None], axis=1)
    everyone = lax.all_to_all(
        jnp.broadcast_to(by_variant[None], (NX * NY, *by_variant.shape)),
        PROMPT, 0, 0, tiled=True,
    )
    square = everyone.sum(axis=0)
    scale = lax.rsqrt(square / D + EPS) * guidance[:, None]
    scale = jnp.sum(placed_at[:, :, None] * scale[:, None], axis=0)
    mixed = (jnp.sum(state * scale[:, :, None], axis=0) * norm_gain).astype(BF)

    peer = shifted(mixed, "c", NC, 1)
    first = jnp.where(c == 0, jnp.stack([mixed, peer]), jnp.stack([peer, mixed]))
    before = shifted(first, "z", NZ, 1)
    after = shifted(first, "z", NZ, -1)
    three = jnp.stack([before, first, after])
    low = shifted(three, "z", NZ, 3)
    high = shifted(three[:2], "z", NZ, -3)
    ring = jnp.concatenate([first[None], after[None], high, low, before[None]])
    rows = jnp.roll(ring, z, axis=0).transpose(1, 0, 2, 3).reshape(-1, share)

    product = jnp.dot(rows, unembed, preferred_element_type=F32).astype(BF)
    tiles = product.reshape(NX * NY, -1, product.shape[-1])
    tiles = lax.all_to_all(tiles, PROMPT, 0, 0, tiled=True)
    scores = jnp.sum(wide(tiles), axis=0) + logit_bias
    top = jnp.max(scores, axis=1, keepdims=True)
    part_lse = top[:, 0] + jnp.log(jnp.sum(jnp.exp(scores - top), axis=1))
    shards = NZ * NW * NC
    part_lse = lax.all_to_all(
        jnp.broadcast_to(part_lse[None, None], (shards, 1, part_lse.shape[0])),
        TENSOR, 0, 0, tiled=True,
    )
    lse = jax.nn.logsumexp(part_lse[:, 0], axis=0)
    return scores - lse[:, None]


def solution(mesh):
    finer = Mesh(mesh.devices.reshape(NX, NY, NZ, NW, NC), AXES)
    placed = (
        P(PROMPT, None, None),
        P(PROMPT, TENSOR),
        P(PROMPT, TENSOR),
        P(TENSOR, PROMPT),
        P(PROMPT),
        P(PROMPT, TENSOR),
        P(),
        P(PROMPT, TENSOR),
    )
    return jax.shard_map(
        local, mesh=finer, in_specs=placed, out_specs=P(PROMPT, TENSOR), check_vma=False
    )
```

```python
import jax
import jax.numpy as jnp
from jax import lax
from jax.sharding import Mesh
from jax.sharding import PartitionSpec as P


D = 8192
EPS = 1e-05
NX, NY, NZ, NW, NC = 4, 2, 8, 2, 2
AXES = ("x", "y", "z", "w", "c")
PROMPT = ("x", "y")
TENSOR = ("z", "w", "c")
BF, F32 = jnp.bfloat16, jnp.float32


def shifted(array, axis, size, step):
    return lax.ppermute(array, axis, [(i, (i + step) % size) for i in range(size)])


def wide(array):
    return array.astype(F32)


def tokens_for_block(tokens, c):
    half = tokens.shape[0] // NC
    share = D // (NX * NY)
    mine = lax.dynamic_slice_in_dim(tokens, c * half, half, 0)
    blocks = mine.reshape(half, NX * NY, share).transpose(1, 0, 2)
    own = lax.all_to_all(blocks, PROMPT, 0, 0, tiled=True)
    other = shifted(own, "c", NC, 1)
    shape = (NX, NY, half, share)
    return own.reshape(shape), other.reshape(shape)


def at(array, index, axis):
    return lax.dynamic_index_in_dim(array, index, axis, keepdims=False)


def products(rows, weights):
    flat = rows.reshape(-1, rows.shape[-1])
    outs = [jnp.dot(flat, weight, preferred_element_type=F32) for weight in weights]
    return [out.reshape(*rows.shape[:-1], -1) for out in outs]


def joined(pair):
    return jnp.stack([part.astype(BF) for part in pair])


def step(tokens, gate_weight, up_weight, down_weight, norm_gain, unembed, guidance, logit_bias):
    x, y, z, _, c = (lax.axis_index(axis) for axis in AXES)
    tokens = tokens[0]
    own, other = tokens_for_block(tokens, c)
    both = (gate_weight, up_weight)

    def toward(d):
        return (x + d) % NX

    pa = products(own, both)
    swap_a = shifted(joined([at(p, 1 - y, 1) for p in pa]), "y", NY, 1)
    pb = products(other, both)
    got_b = [shifted(joined([at(p, toward(d), 0) for p in pb]), "x", NX, d) for d in (2, 1, 3)]
    swap_a, got_b = lax.optimization_barrier((swap_a, got_b))
    sum_a = [at(p, y, 1) + wide(got) for p, got in zip(pa, swap_a)]
    got_a = [shifted(joined([at(p, toward(d), 0) for p in sum_a]), "x", NX, d) for d in (2, 1, 3)]
    sum_b = [at(p, x, 0) + sum(wide(got[i]) for got in got_b) for i, p in enumerate(pb)]
    swap_b = shifted(joined([at(p, 1 - y, 0) for p in sum_b]), "y", NY, 1)
    gate_b, up_b = [at(p, y, 0) + wide(got) for p, got in zip(sum_b, swap_b)]
    hidden_b = (jax.nn.silu(gate_b) * up_b).astype(BF)
    gate_a, up_a = [at(p, x, 0) + sum(wide(g[i]) for g in got_a) for i, p in enumerate(sum_a)]
    hidden_a = (jax.nn.silu(gate_a) * up_a).astype(BF)

    line_b = [hidden_b] + [None] * (NX - 1)
    for d in (2, 1, 3):
        line_b[d] = shifted(hidden_b, "x", NX, -d)
    line_b = jnp.stack(line_b)
    all_b = jnp.stack([line_b, shifted(line_b, "y", NY, 1)], axis=1)
    pair_a = jnp.stack([hidden_a, shifted(hidden_a, "y", NY, 1)])
    all_a = [pair_a] + [None] * (NX - 1)
    for d in (2, 1, 3):
        all_a[d] = shifted(pair_a, "x", NX, -d)
    all_a = jnp.stack(all_a)

    (down_b,) = products(all_b, (down_weight,))
    passed = shifted(down_b.astype(BF), "c", NC, 1)
    (down_a,) = products(all_a, (down_weight,))
    share = down_a.shape[-1]
    part = down_a + wide(passed)
    part = part.reshape(NX * NY, NZ, -1, share)

    def piece(k):
        return lax.dynamic_index_in_dim(part, (z + k) % NZ, 1, keepdims=False)

    def sent(block, step):
        return shifted(block.astype(BF), "z", NZ, step)

    far = sent(piece(4), 4)
    relay_up, relay_down = sent(piece(3), 1), sent(piece(5), -1)
    one_up, one_down = sent(piece(1), 1), sent(piece(7), -1)
    two_up = sent(piece(2) + wide(relay_up), 2)
    two_down = sent(piece(6) + wide(relay_down), -2)
    mine = piece(0) + sum(wide(got) for got in (far, one_up, one_down, two_up, two_down))
    mine = mine.astype(BF)
    branch = wide(mine) + wide(shifted(mine, "w", NW, 1))

    residual = at(own.reshape(NX, NY, NZ, -1, share), z, 2)
    residual = jnp.concatenate([residual, residual])
    residual = lax.dynamic_slice_in_dim(residual, x, NX, 0)
    residual = jnp.where(y == 0, residual, residual[:, ::-1]).reshape(NX * NY, -1, share)
    state = wide(residual) + branch
    partial_square = jnp.sum(state * state, axis=2)
    offsets = jnp.arange(NX * NY)
    variant_at = ((x + offsets // NY) % NX) * NY + ((offsets % NY) ^ y)
    placed_at = (variant_at[None, :] == offsets[:, None]).astype(F32)
    by_variant = jnp.sum(placed_at[:, :, None] * partial_square[None], axis=1)
    everyone = lax.all_to_all(
        jnp.broadcast_to(by_variant[None], (NX * NY, *by_variant.shape)),
        PROMPT, 0, 0, tiled=True,
    )
    square = everyone.sum(axis=0)
    scale = lax.rsqrt(square / D + EPS) * guidance[:, None]
    scale = jnp.sum(placed_at[:, :, None] * scale[:, None], axis=0)
    mixed = (jnp.sum(state * scale[:, :, None], axis=0) * norm_gain).astype(BF)

    before = shifted(mixed, "z", NZ, 1)
    after = shifted(mixed, "z", NZ, -1)
    three = jnp.stack([before, mixed, after])
    low = shifted(three, "z", NZ, 3)
    high = shifted(three[:2], "z", NZ, -3)
    ring = jnp.concatenate([mixed[None], after[None], high, low, before[None]])
    ring = jnp.roll(ring, z, axis=0).reshape(-1, share)
    peer = shifted(ring, "c", NC, 1)
    first = jnp.where(c == 0, ring, peer)
    second = jnp.where(c == 0, peer, ring)
    rows = jnp.concatenate([first, second])

    product = jnp.dot(rows, unembed, preferred_element_type=F32).astype(BF)
    tiles = product.reshape(NX * NY, -1, product.shape[-1])
    tiles = lax.all_to_all(tiles, PROMPT, 0, 0, tiled=True)
    scores = jnp.sum(wide(tiles), axis=0) + logit_bias
    top = jnp.max(scores, axis=1, keepdims=True)
    part_lse = top[:, 0] + jnp.log(jnp.sum(jnp.exp(scores - top), axis=1))
    shards = NZ * NW * NC
    part_lse = lax.all_to_all(
        jnp.broadcast_to(part_lse[None, None], (shards, 1, part_lse.shape[0])),
        TENSOR, 0, 0, tiled=True,
    )
    lse = jax.nn.logsumexp(part_lse[:, 0], axis=0)
    return scores - lse[:, None]


def solution(mesh):
    finer = Mesh(mesh.devices.reshape(NX, NY, NZ, NW, NC), AXES)
    placed = (
        P(PROMPT, None, None),
        P(PROMPT, TENSOR),
        P(PROMPT, TENSOR),
        P(TENSOR, PROMPT),
        P(PROMPT),
        P(PROMPT, TENSOR),
        P(),
        P(PROMPT, TENSOR),
    )
    return jax.shard_map(
        step, mesh=finer, in_specs=placed, out_specs=P(PROMPT, TENSOR), check_vma=False
    )
```

```python
import jax
import jax.numpy as jnp
from jax import lax
from jax.sharding import Mesh
from jax.sharding import PartitionSpec as P


D = 8192
EPS = 1e-05
NX, NY, NZ, NW, NC = 4, 2, 8, 2, 2
AXES = ("x", "y", "z", "w", "c")
PROMPT = ("x", "y")
TENSOR = ("z", "w", "c")
BF, F32 = jnp.bfloat16, jnp.float32


def shifted(array, axis, size, step):
    return lax.ppermute(array, axis, [(i, (i + step) % size) for i in range(size)])


def paired(array, axis, size, bit):
    return lax.ppermute(array, axis, [(i, i ^ bit) for i in range(size)])


def flipped_if(bit, array, axis):
    return jnp.where(bit == 0, array, jnp.flip(array, axis))


def wide(array):
    return array.astype(F32)


def tokens_for_block(tokens, x, y, c):
    half = tokens.shape[0] // NC
    share = D // (NX * NY)
    mine = lax.dynamic_slice_in_dim(tokens, c * half, half, 0)
    blocks = mine.reshape(half, NX * NY, share).transpose(1, 0, 2)
    own = lax.all_to_all(blocks, PROMPT, 0, 0, tiled=True)
    own = own.reshape(2, 2, NY, half, share)
    for axis, bit in enumerate((x // 2, x % 2, y)):
        own = flipped_if(bit, own, axis)
    own = lax.optimization_barrier(own.reshape(NX, NY, half, share))
    return own, paired(own, "c", NC, 1)


def at(array, index, axis):
    return lax.dynamic_index_in_dim(array, index, axis, keepdims=False)


def products(rows, weights):
    flat = rows.reshape(-1, rows.shape[-1])
    outs = [jnp.dot(flat, weight, preferred_element_type=F32) for weight in weights]
    return [out.reshape(*rows.shape[:-1], -1) for out in outs]


def joined(pair):
    return jnp.stack([part.astype(BF) for part in pair])


def step(tokens, gate_weight, up_weight, down_weight, norm_gain, unembed, guidance, logit_bias):
    x, y, z, _, c = (lax.axis_index(axis) for axis in AXES)
    tokens = tokens[0]
    own, other = tokens_for_block(tokens, x, y, c)
    both = (gate_weight, up_weight)

    pa = products(own, both)
    got_a = [paired(joined([p[d] for p in pa]), "x", NX, d) for d in TURNS]
    pb = products(other, both)
    swap_b = paired(joined([p[:, 1] for p in pb]), "y", NY, 1)
    got_a, swap_b = lax.optimization_barrier((got_a, swap_b))
    sum_a = [p[0] + sum(wide(got[i]) for got in got_a) for i, p in enumerate(pa)]
    swap_a = paired(joined([p[1] for p in sum_a]), "y", NY, 1)
    sum_b = [p[:, 0] + wide(got) for p, got in zip(pb, swap_b)]
    got_b = [paired(joined([p[d] for p in sum_b]), "x", NX, d) for d in TURNS]
    gate_a, up_a = [p[0] + wide(got) for p, got in zip(sum_a, swap_a)]
    hidden_a = (jax.nn.silu(gate_a) * up_a).astype(BF)
    gate_b, up_b = [p[0] + sum(wide(got[i]) for got in got_b) for i, p in enumerate(sum_b)]
    hidden_b = (jax.nn.silu(gate_b) * up_b).astype(BF)

    line_a = [hidden_a] + [None] * (NX - 1)
    for d in TURNS:
        line_a[d] = paired(hidden_a, "x", NX, d)
    line_a = jnp.stack(line_a)
    all_a = jnp.stack([line_a, paired(line_a, "y", NY, 1)], axis=1)
    pair_b = jnp.stack([hidden_b, paired(hidden_b, "y", NY, 1)])
    all_b = [pair_b] + [None] * (NX - 1)
    for d in TURNS:
        all_b[d] = paired(pair_b, "x", NX, d)
    all_b = jnp.stack(all_b)

    (down_a,) = products(all_a, (down_weight,))
    passed = paired(down_a.astype(BF), "c", NC, 1)
    (down_b,) = products(all_b, (down_weight,))
    part = down_b + wide(passed)
    share = part.shape[-1]
    part = part.reshape(NX * NY, NZ, -1, share)

    def piece(k):
        return lax.dynamic_index_in_dim(part, (z + k) % NZ, 1, keepdims=False)

    def sent(block, step):
        return shifted(block.astype(BF), "z", NZ, step)

    far = sent(piece(4), 4)
    relay_up, relay_down = sent(piece(3), 1), sent(piece(5), -1)
    one_up, one_down = sent(piece(1), 1), sent(piece(7), -1)
    two_up = sent(piece(2) + wide(relay_up), 2)
    two_down = sent(piece(6) + wide(relay_down), -2)
    mine = piece(0) + sum(wide(got) for got in (far, one_up, one_down, two_up, two_down))
    mine = mine.astype(BF)
    branch = wide(mine) + wide(shifted(mine, "w", NW, 1))

    residual = at(other.reshape(NX * NY, NZ, -1, share), z, 1)
    state = wide(residual) + branch
    partial_square = jnp.sum(state * state, axis=2)
    offsets = jnp.arange(NX * NY)
    variant_at = offsets ^ (x * NY + y)
    placed_at = (variant_at[None, :] == offsets[:, None]).astype(F32)
    by_variant = jnp.sum(placed_at[:, :, None] * partial_square[None], axis=1)
    everyone = lax.all_to_all(
        jnp.broadcast_to(by_variant[None], (NX * NY, *by_variant.shape)),
        PROMPT, 0, 0, tiled=True,
    )
    square = everyone.sum(axis=0)
    scale = lax.rsqrt(square / D + EPS) * guidance[:, None]
    scale = jnp.sum(placed_at[:, :, None] * scale[:, None], axis=0)
    mixed = (jnp.sum(state * scale[:, :, None], axis=0) * norm_gain).astype(BF)

    ring = mixed
    for bit in (1, 2, 4):
        peer = paired(ring, "z", NZ, bit)
        low = (z & bit) == 0
        ring = jnp.concatenate([jnp.where(low, ring, peer), jnp.where(low, peer, ring)])
    peer = paired(ring, "c", NC, 1)
    first = jnp.where(c == 0, peer, ring)
    second = jnp.where(c == 0, ring, peer)
    rows = jnp.concatenate([first, second])

    product = jnp.dot(rows, unembed, preferred_element_type=F32).astype(BF)
    tiles = product.reshape(NX * NY, -1, product.shape[-1])
    tiles = lax.all_to_all(tiles, PROMPT, 0, 0, tiled=True)
    scores = jnp.sum(wide(tiles), axis=0) + logit_bias
    top = jnp.max(scores, axis=1, keepdims=True)
    part_lse = top[:, 0] + jnp.log(jnp.sum(jnp.exp(scores - top), axis=1))
    shards = NZ * NW * NC
    part_lse = lax.all_to_all(
        jnp.broadcast_to(part_lse[None, None], (shards, 1, part_lse.shape[0])),
        TENSOR, 0, 0, tiled=True,
    )
    lse = jax.nn.logsumexp(part_lse[:, 0], axis=0)
    return scores - lse[:, None]


TURNS = (2, 1, 3)


def solution(mesh):
    finer = Mesh(mesh.devices.reshape(NX, NY, NZ, NW, NC), AXES)
    placed = (
        P(PROMPT, None, None),
        P(PROMPT, TENSOR),
        P(PROMPT, TENSOR),
        P(TENSOR, PROMPT),
        P(PROMPT),
        P(PROMPT, TENSOR),
        P(),
        P(PROMPT, TENSOR),
    )
    return jax.shard_map(
        step, mesh=finer, in_specs=placed, out_specs=P(PROMPT, TENSOR), check_vma=False
    )
```

```python
import jax
import jax.numpy as jnp
from jax import lax
from jax.experimental import pallas as pl
from jax.experimental.pallas import tpu as pltpu
from jax.sharding import Mesh
from jax.sharding import PartitionSpec as P


D = 8192
EPS = 1e-05
NX, NY, NZ, NW, NC = 4, 2, 8, 2, 2
AXES = ("x", "y", "z", "w", "c")
PROMPT = ("x", "y")
TENSOR = ("z", "w", "c")
BF, F32 = jnp.bfloat16, jnp.float32


def shifted(array, axis, size, step):
    return lax.ppermute(array, axis, [(i, (i + step) % size) for i in range(size)])


def paired(array, axis, size, bit):
    return lax.ppermute(array, axis, [(i, i ^ bit) for i in range(size)])


def wide(array):
    return array.astype(F32)


def paired_prompt(array, k):
    return lax.ppermute(array, PROMPT, [(p, p ^ k) for p in range(NX * NY)])


def blocks_kernel(place_ref, rows_ref, out_ref):
    share = out_ref.shape[2]
    for k in range(NX * NY):
        start = pl.multiple_of((place_ref[0] ^ k) * share, share)
        out_ref[k] = rows_ref[:, pl.ds(start, share)]


def blocks_for(tokens, place, c):
    half = tokens.shape[0] // NC
    share = D // (NX * NY)
    return pl.pallas_call(
        blocks_kernel,
        out_shape=jax.ShapeDtypeStruct((NX * NY, half, share), tokens.dtype),
        grid_spec=pltpu.PrefetchScalarGridSpec(
            num_scalar_prefetch=1,
            grid=(1,),
            in_specs=[pl.BlockSpec((half, D), lambda i, where: (where[1], 0))],
            out_specs=pl.BlockSpec((NX * NY, half, share), lambda i, where: (0, 0, 0)),
        ),
    )(jnp.stack([place, c]).astype(jnp.int32), tokens)


def tokens_for_block(tokens, place, c):
    blocks = blocks_for(tokens, place, c)
    own = [blocks[0]] + [None] * (NX * NY - 1)
    for k in (4, 5, 2, 3, 6, 7, 1):
        own[k] = paired_prompt(blocks[k], k)
    other = paired(jnp.stack(own), "c", NC, 1)
    return own, other.reshape(NX, NY, *own[0].shape)


def at(array, index, axis):
    return lax.dynamic_index_in_dim(array, index, axis, keepdims=False)


def products(rows, weights):
    flat = rows.reshape(-1, rows.shape[-1])
    outs = [jnp.dot(flat, weight, preferred_element_type=F32) for weight in weights]
    return [out.reshape(*rows.shape[:-1], -1) for out in outs]


def joined(pair):
    return jnp.stack([part.astype(BF) for part in pair])


def step(tokens, gate_weight, up_weight, down_weight, norm_gain, unembed, guidance, logit_bias):
    x, y, z, _, c = (lax.axis_index(axis) for axis in AXES)
    tokens = tokens[0]
    own, other = tokens_for_block(tokens, x * NY + y, c)
    both = (gate_weight, up_weight)

    def own_products(*offsets):
        rows = jnp.stack([jnp.stack(own[NY * d : NY * d + NY]) for d in offsets])
        return zip(offsets, zip(*products(rows, both)))

    pa, got_a = {}, []
    for offsets in ((2,), (1, 3), (0,)):
        pa.update(own_products(*offsets))
    got_a = [paired(joined(pa[d]), "x", NX, d) for d in TURNS]
    pb = products(other, both)
    swap_b = paired(joined([p[1:, 1] for p in pb]), "y", NY, 1)
    got_a, swap_b, pa[0] = lax.optimization_barrier((got_a, swap_b, pa[0]))
    sum_a = [p + sum(wide(got[i]) for got in got_a) for i, p in enumerate(pa[0])]
    swap_a = paired(joined([p[1] for p in sum_a]), "y", NY, 1)
    sum_b = [p[1:, 0] + wide(got) for p, got in zip(pb, swap_b)]
    got_b = [paired(joined([p[d - 1] for p in sum_b]), "x", NX, d) for d in TURNS]
    last_b = paired(joined([p[0, 1] for p in pb]), "y", NY, 1)
    got_b = got_b + [last_b]
    gate_a, up_a = [p[0] + wide(got) for p, got in zip(sum_a, swap_a)]
    hidden_a = (jax.nn.silu(gate_a) * up_a).astype(BF)
    gate_b, up_b = [p[0, 0] + sum(wide(got[i]) for got in got_b) for i, p in enumerate(pb)]
    hidden_b = (jax.nn.silu(gate_b) * up_b).astype(BF)

    line_a = [hidden_a] + [None] * (NX - 1)
    for d in TURNS:
        line_a[d] = paired(hidden_a, "x", NX, d)
    line_a = jnp.stack(line_a)
    all_a = jnp.stack([line_a, paired(line_a, "y", NY, 1)], axis=1)
    pair_b = jnp.stack([hidden_b, paired(hidden_b, "y", NY, 1)])
    all_b = [pair_b] + [None] * (NX - 1)
    for d in TURNS:
        all_b[d] = paired(pair_b, "x", NX, d)
    all_b = jnp.stack(all_b)

    (down_a,) = products(all_a, (down_weight,))
    passed = paired(down_a.astype(BF), "c", NC, 1)
    (down_b,) = products(all_b, (down_weight,))
    part = down_b + wide(passed)
    share = part.shape[-1]
    part = part.reshape(NX * NY, NZ, -1, share)

    def piece(k):
        return lax.dynamic_index_in_dim(part, (z + k) % NZ, 1, keepdims=False)

    def sent(block, step):
        return shifted(block.astype(BF), "z", NZ, step)

    far = sent(piece(4), 4)
    relay_up, relay_down = sent(piece(3), 1), sent(piece(5), -1)
    one_up, one_down = sent(piece(1), 1), sent(piece(7), -1)
    two_up = sent(piece(2) + wide(relay_up), 2)
    two_down = sent(piece(6) + wide(relay_down), -2)
    mine = piece(0) + sum(wide(got) for got in (far, one_up, one_down, two_up, two_down))
    mine = mine.astype(BF)
    branch = wide(mine) + wide(shifted(mine, "w", NW, 1))

    residual = at(other.reshape(NX * NY, NZ, -1, share), z, 1)
    state = wide(residual) + branch
    partial_square = jnp.sum(state * state, axis=2)
    offsets = jnp.arange(NX * NY)
    variant_at = offsets ^ (x * NY + y)
    placed_at = (variant_at[None, :] == offsets[:, None]).astype(F32)
    by_variant = jnp.sum(placed_at[:, :, None] * partial_square[None], axis=1)
    everyone = lax.all_to_all(
        jnp.broadcast_to(by_variant[None], (NX * NY, *by_variant.shape)),
        PROMPT, 0, 0, tiled=True,
    )
    square = everyone.sum(axis=0)
    scale = lax.rsqrt(square / D + EPS) * guidance[:, None]
    scale = jnp.sum(placed_at[:, :, None] * scale[:, None], axis=0)
    mixed = (jnp.sum(state * scale[:, :, None], axis=0) * norm_gain).astype(BF)

    ring = jnp.broadcast_to(mixed[None], (NZ, *mixed.shape))
    ring = lax.all_to_all(ring, "z", 0, 0, tiled=True).reshape(-1, share)
    peer = paired(ring, "c", NC, 1)
    first = jnp.where(c == 0, peer, ring)
    second = jnp.where(c == 0, ring, peer)
    rows = jnp.concatenate([first, second])

    product = jnp.dot(rows, unembed, preferred_element_type=F32).astype(BF)
    tiles = product.reshape(NX * NY, -1, product.shape[-1])
    tiles = lax.all_to_all(tiles, PROMPT, 0, 0, tiled=True)
    scores = jnp.sum(wide(tiles), axis=0) + logit_bias
    top = jnp.max(scores, axis=1, keepdims=True)
    part_lse = top[:, 0] + jnp.log(jnp.sum(jnp.exp(scores - top), axis=1))
    shards = NZ * NW * NC
    part_lse = lax.all_to_all(
        jnp.broadcast_to(part_lse[None, None], (shards, 1, part_lse.shape[0])),
        TENSOR, 0, 0, tiled=True,
    )
    lse = jax.nn.logsumexp(part_lse[:, 0], axis=0)
    return scores - lse[:, None]


TURNS = (2, 1, 3)
TURNS = (2, 1, 3)


def solution(mesh):
    finer = Mesh(mesh.devices.reshape(NX, NY, NZ, NW, NC), AXES)
    placed = (
        P(PROMPT, None, None),
        P(PROMPT, TENSOR),
        P(PROMPT, TENSOR),
        P(TENSOR, PROMPT),
        P(PROMPT),
        P(PROMPT, TENSOR),
        P(),
        P(PROMPT, TENSOR),
    )
    return jax.shard_map(
        step, mesh=finer, in_specs=placed, out_specs=P(PROMPT, TENSOR), check_vma=False
    )
```

```python
import jax
import jax.numpy as jnp
from jax import lax
from jax.experimental import pallas as pl
from jax.sharding import Mesh
from jax.sharding import PartitionSpec as P


D = 8192
EPS = 1e-05
NX, NY, NZ, NW, NC = 4, 2, 8, 2, 2
AXES = ("x", "y", "z", "w", "c")
PROMPT = ("x", "y")
TENSOR = ("z", "w", "c")
BF, F32 = jnp.bfloat16, jnp.float32


def shifted(array, axis, size, step):
    return lax.ppermute(array, axis, [(i, (i + step) % size) for i in range(size)])


def paired(array, axis, size, bit):
    return lax.ppermute(array, axis, [(i, i ^ bit) for i in range(size)])


def wide(array):
    return array.astype(F32)


def paired_prompt(array, k):
    return lax.ppermute(array, PROMPT, [(p, p ^ k) for p in range(NX * NY)])


def blocks_kernel(tokens_ref, *out_refs):
    place = lax.axis_index("x") * NY + lax.axis_index("y")
    half, share = out_refs[0].shape
    first = pl.multiple_of(lax.axis_index("c") * half, half)
    for k, out_ref in enumerate(out_refs):
        start = pl.multiple_of((place ^ k) * share, share)
        out_ref[...] = tokens_ref[pl.ds(first, half), pl.ds(start, share)]


def tokens_for_block(tokens):
    count = NX * NY
    block = jax.ShapeDtypeStruct((tokens.shape[0] // NC, D // count), tokens.dtype)
    own = pl.pallas_call(blocks_kernel, out_shape=[block] * count)(tokens)
    own = list(own)
    for k in (4, 5, 2, 3, 6, 7, 1):
        own[k] = paired_prompt(own[k], k)
    own = jnp.stack(own)
    other = paired(own, "c", NC, 1)
    return [rows.reshape(NX, NY, *block.shape) for rows in (own, other)]


def at(array, index, axis):
    return lax.dynamic_index_in_dim(array, index, axis, keepdims=False)


def products(rows, weights):
    flat = rows.reshape(-1, rows.shape[-1])
    outs = [jnp.dot(flat, weight, preferred_element_type=F32) for weight in weights]
    return [out.reshape(*rows.shape[:-1], -1) for out in outs]


def joined(pair):
    return jnp.stack([part.astype(BF) for part in pair])


def step(tokens, gate_weight, up_weight, down_weight, norm_gain, unembed, guidance, logit_bias):
    x, y, z, _, c = (lax.axis_index(axis) for axis in AXES)
    tokens = tokens[0]
    own, other = tokens_for_block(tokens)
    both = (gate_weight, up_weight)

    pb = products(own, both)
    swap_b = paired(joined([p[:, 1] for p in pb]), "y", NY, 1)
    pa = products(other, both)
    packed_a = [joined([p[d] for p in pa]) for d in TURNS]
    got_a = [paired(packed, "x", NX, d) for d, packed in zip(TURNS, packed_a)]
    sum_a = [p[0] + sum(wide(got[i]) for got in got_a) for i, p in enumerate(pa)]
    swap_a = paired(joined([p[1] for p in sum_a]), "y", NY, 1)
    sum_b = [p[:, 0] + wide(got) for p, got in zip(pb, swap_b)]
    got_b = [paired(joined([p[d] for p in sum_b]), "x", NX, d) for d in TURNS]
    gate_a, up_a = [p[0] + wide(got) for p, got in zip(sum_a, swap_a)]
    hidden_a = (jax.nn.silu(gate_a) * up_a).astype(BF)
    gate_b, up_b = [p[0] + sum(wide(got[i]) for got in got_b) for i, p in enumerate(sum_b)]
    hidden_b = (jax.nn.silu(gate_b) * up_b).astype(BF)

    line_a = [hidden_a] + [None] * (NX - 1)
    for d in TURNS:
        line_a[d] = paired(hidden_a, "x", NX, d)
    line_a = jnp.stack(line_a)
    all_a = jnp.stack([line_a, paired(line_a, "y", NY, 1)], axis=1)
    pair_b = jnp.stack([hidden_b, paired(hidden_b, "y", NY, 1)])
    all_b = [pair_b] + [None] * (NX - 1)
    for d in TURNS:
        all_b[d] = paired(pair_b, "x", NX, d)
    all_b = jnp.stack(all_b)

    (down_a,) = products(all_a, (down_weight,))
    passed = paired(down_a.astype(BF), "c", NC, 1)
    (down_b,) = products(all_b, (down_weight,))
    part = (down_b + wide(passed)).astype(BF)
    share = part.shape[-1]
    part = part.reshape(NX * NY, NZ, -1, share)

    def piece(k):
        return lax.dynamic_index_in_dim(part, (z + k) % NZ, 1, keepdims=False)

    def sent(block, step):
        return shifted(block.astype(BF), "z", NZ, step)

    far = sent(piece(4), 4)
    relay_up, relay_down = sent(piece(3), 1), sent(piece(5), -1)
    one_up, one_down = sent(piece(1), 1), sent(piece(7), -1)
    two_up = sent(wide(piece(2)) + wide(relay_up), 2)
    two_down = sent(wide(piece(6)) + wide(relay_down), -2)
    mine = wide(piece(0)) + sum(wide(got) for got in (far, one_up, one_down, two_up, two_down))
    mine = mine.astype(BF)
    branch = wide(mine) + wide(shifted(mine, "w", NW, 1))

    residual = at(own.reshape(NX * NY, NZ, -1, share), z, 1)
    state = wide(residual) + branch
    partial_square = jnp.sum(state * state, axis=2)
    offsets = jnp.arange(NX * NY)
    variant_at = offsets ^ (x * NY + y)
    placed_at = (variant_at[None, :] == offsets[:, None]).astype(F32)
    by_variant = jnp.sum(placed_at[:, :, None] * partial_square[None], axis=1)
    everyone = lax.all_to_all(
        jnp.broadcast_to(by_variant[None], (NX * NY, *by_variant.shape)),
        PROMPT, 0, 0, tiled=True,
    )
    square = everyone.sum(axis=0)
    scale = lax.rsqrt(square / D + EPS) * guidance[:, None]
    scale = jnp.sum(placed_at[:, :, None] * scale[:, None], axis=0)
    mixed = (jnp.sum(state * scale[:, :, None], axis=0) * norm_gain).astype(BF)

    ring = jnp.broadcast_to(mixed[None], (NZ, *mixed.shape))
    ring = lax.all_to_all(ring, "z", 0, 0, tiled=True).reshape(-1, share)
    peer = paired(ring, "c", NC, 1)
    first = jnp.where(c == 0, ring, peer)
    second = jnp.where(c == 0, peer, ring)
    rows = jnp.concatenate([first, second])

    product = jnp.dot(rows, unembed, preferred_element_type=F32).astype(BF)
    tiles = product.reshape(NX * NY, -1, product.shape[-1])
    tiles = lax.all_to_all(tiles, PROMPT, 0, 0, tiled=True)
    scores = jnp.sum(wide(tiles), axis=0) + logit_bias
    top = jnp.max(scores, axis=1, keepdims=True)
    part_lse = top[:, 0] + jnp.log(jnp.sum(jnp.exp(scores - top), axis=1))
    shards = NZ * NW * NC
    part_lse = lax.all_to_all(
        jnp.broadcast_to(part_lse[None, None], (shards, 1, part_lse.shape[0])),
        TENSOR, 0, 0, tiled=True,
    )
    lse = jax.nn.logsumexp(part_lse[:, 0], axis=0)
    return scores - lse[:, None]


TURNS = (2, 1, 3)
TURNS = (2, 1, 3)


def solution(mesh):
    finer = Mesh(mesh.devices.reshape(NX, NY, NZ, NW, NC), AXES)
    placed = (
        P(PROMPT, None, None),
        P(PROMPT, TENSOR),
        P(PROMPT, TENSOR),
        P(TENSOR, PROMPT),
        P(PROMPT),
        P(PROMPT, TENSOR),
        P(),
        P(PROMPT, TENSOR),
    )
    return jax.shard_map(
        step, mesh=finer, in_specs=placed, out_specs=P(PROMPT, TENSOR), check_vma=False
    )
```

```python
import jax
import jax.numpy as jnp
from jax import lax
from jax.experimental import pallas as pl
from jax.sharding import Mesh
from jax.sharding import PartitionSpec as P


D = 8192
EPS = 1e-05
NX, NY, NZ, NW, NC = 4, 2, 8, 2, 2
AXES = ("x", "y", "z", "w", "c")
PROMPT = ("x", "y")
TENSOR = ("z", "w", "c")
BF, F32 = jnp.bfloat16, jnp.float32


def shifted(array, axis, size, step):
    return lax.ppermute(array, axis, [(i, (i + step) % size) for i in range(size)])


def paired(array, axis, size, bit):
    return lax.ppermute(array, axis, [(i, i ^ bit) for i in range(size)])


def wide(array):
    return array.astype(F32)


def paired_prompt(array, k):
    return lax.ppermute(array, PROMPT, [(p, p ^ k) for p in range(NX * NY)])


def blocks_kernel(tokens_ref, *out_refs):
    place = lax.axis_index("x") * NY + lax.axis_index("y")
    half, share = out_refs[0].shape
    first = pl.multiple_of(lax.axis_index("c") * half, half)
    for k, out_ref in enumerate(out_refs):
        start = pl.multiple_of((place ^ k) * share, share)
        out_ref[...] = tokens_ref[pl.ds(first, half), pl.ds(start, share)]


def tokens_for_block(tokens):
    count = NX * NY
    block = jax.ShapeDtypeStruct((tokens.shape[0] // NC, D // count), tokens.dtype)
    own = pl.pallas_call(blocks_kernel, out_shape=[block] * count)(tokens)
    own = list(own)
    for k in (4, 5, 2, 3, 6, 7, 1):
        own[k] = paired_prompt(own[k], k)
    own = jnp.stack(own)
    other = paired(own, "c", NC, 1)
    return [rows.reshape(NX, NY, *block.shape) for rows in (own, other)]


def at(array, index, axis):
    return lax.dynamic_index_in_dim(array, index, axis, keepdims=False)


def products(rows, weights):
    flat = rows.reshape(-1, rows.shape[-1])
    outs = [jnp.dot(flat, weight, preferred_element_type=F32) for weight in weights]
    return [out.reshape(*rows.shape[:-1], -1) for out in outs]


def joined(pair):
    return jnp.stack([part.astype(BF) for part in pair])


def step(tokens, gate_weight, up_weight, down_weight, norm_gain, unembed, guidance, logit_bias):
    x, y, z, _, c = (lax.axis_index(axis) for axis in AXES)
    tokens = tokens[0]
    own, other = tokens_for_block(tokens)
    both = (gate_weight, up_weight)

    pb = products(own, both)
    swap_b = paired(joined([p[:, 1] for p in pb]), "y", NY, 1)
    pa = products(other, both)
    packed_a = [joined([p[d] for p in pa]) for d in TURNS]
    got_a = [paired(packed, "x", NX, d) for d, packed in zip(TURNS, packed_a)]
    sum_a = [p[0] + sum(wide(got[i]) for got in got_a) for i, p in enumerate(pa)]
    swap_a = paired(joined([p[1] for p in sum_a]), "y", NY, 1)
    sum_b = [p[:, 0] + wide(got) for p, got in zip(pb, swap_b)]
    got_b = [paired(joined([p[d] for p in sum_b]), "x", NX, d) for d in TURNS]
    gate_a, up_a = [p[0] + wide(got) for p, got in zip(sum_a, swap_a)]
    hidden_a = (jax.nn.silu(gate_a) * up_a).astype(BF)
    gate_b, up_b = [p[0] + sum(wide(got[i]) for got in got_b) for i, p in enumerate(sum_b)]
    hidden_b = (jax.nn.silu(gate_b) * up_b).astype(BF)

    line_a = [hidden_a] + [None] * (NX - 1)
    for d in TURNS:
        line_a[d] = paired(hidden_a, "x", NX, d)
    line_a = jnp.stack(line_a)
    all_a = jnp.stack([line_a, paired(line_a, "y", NY, 1)], axis=1)
    pair_b = jnp.stack([hidden_b, paired(hidden_b, "y", NY, 1)])
    all_b = [pair_b] + [None] * (NX - 1)
    for d in TURNS:
        all_b[d] = paired(pair_b, "x", NX, d)
    all_b = jnp.stack(all_b)

    (down_a,) = products(all_a, (down_weight,))
    passed = paired(down_a.astype(BF), "c", NC, 1)
    (down_b,) = products(all_b, (down_weight,))
    part = (down_b + wide(passed)).astype(BF)
    share = part.shape[-1]
    part = part.reshape(NX * NY, NZ, -1, share)

    def piece(k):
        return lax.dynamic_index_in_dim(part, (z + k) % NZ, 1, keepdims=False)

    def sent(block, step):
        return shifted(block, "z", NZ, step)

    cut = NX * NY // 2
    far = piece(4)
    far_up, far_down = sent(far[:cut], 2), sent(far[cut:], -2)
    relay_up, relay_down = sent(piece(3), 1), sent(piece(5), -1)
    two_up = wide(piece(2)) + wide(relay_up)
    two_up = jnp.concatenate([two_up[:cut] + wide(far_up), two_up[cut:]]).astype(BF)
    two_down = wide(piece(6)) + wide(relay_down)
    two_down = jnp.concatenate([two_down[:cut], two_down[cut:] + wide(far_down)]).astype(BF)
    two_up, two_down = sent(two_up, 2), sent(two_down, -2)
    one_up, one_down = sent(piece(1), 1), sent(piece(7), -1)
    mine = wide(piece(0)) + sum(wide(got) for got in (one_up, one_down, two_up, two_down))
    mine = mine.astype(BF)
    branch = wide(mine) + wide(shifted(mine, "w", NW, 1))

    residual = at(own.reshape(NX * NY, NZ, -1, share), z, 1)
    state = wide(residual) + branch
    partial_square = jnp.sum(state * state, axis=2)
    offsets = jnp.arange(NX * NY)
    variant_at = offsets ^ (x * NY + y)
    placed_at = (variant_at[None, :] == offsets[:, None]).astype(F32)
    by_variant = jnp.sum(placed_at[:, :, None] * partial_square[None], axis=1)
    square = by_variant + paired(by_variant, "y", NY, 1)
    square = square + sum([paired(square, "x", NX, d) for d in TURNS])
    scale = lax.rsqrt(square / D + EPS) * guidance[:, None]
    scale = jnp.sum(placed_at[:, :, None] * scale[:, None], axis=0)
    mixed = (jnp.sum(state * scale[:, :, None], axis=0) * norm_gain).astype(BF)

    ring = jnp.broadcast_to(mixed[None], (NZ, *mixed.shape))
    ring = lax.all_to_all(ring, "z", 0, 0, tiled=True).reshape(-1, share)
    peer = paired(ring, "c", NC, 1)
    first = jnp.where(c == 0, ring, peer)
    second = jnp.where(c == 0, peer, ring)
    rows = jnp.concatenate([first, second])

    product = jnp.dot(rows, unembed, preferred_element_type=F32).astype(BF)
    tiles = product.reshape(NX * NY, -1, product.shape[-1])
    tiles = lax.all_to_all(tiles, PROMPT, 0, 0, tiled=True)
    scores = jnp.sum(wide(tiles), axis=0) + logit_bias
    top = jnp.max(scores, axis=1, keepdims=True)
    part_lse = top[:, 0] + jnp.log(jnp.sum(jnp.exp(scores - top), axis=1))
    shards = NZ * NW * NC
    part_lse = lax.all_to_all(
        jnp.broadcast_to(part_lse[None, None], (shards, 1, part_lse.shape[0])),
        TENSOR, 0, 0, tiled=True,
    )
    lse = jax.nn.logsumexp(part_lse[:, 0], axis=0)
    return scores - lse[:, None]


TURNS = (2, 1, 3)
TURNS = (2, 1, 3)


def solution(mesh):
    finer = Mesh(mesh.devices.reshape(NX, NY, NZ, NW, NC), AXES)
    placed = (
        P(PROMPT, None, None),
        P(PROMPT, TENSOR),
        P(PROMPT, TENSOR),
        P(TENSOR, PROMPT),
        P(PROMPT),
        P(PROMPT, TENSOR),
        P(),
        P(PROMPT, TENSOR),
    )
    return jax.shard_map(
        step, mesh=finer, in_specs=placed, out_specs=P(PROMPT, TENSOR), check_vma=False
    )
```

```python
import jax
import jax.numpy as jnp
from jax import lax
from jax.experimental import pallas as pl
from jax.sharding import Mesh
from jax.sharding import PartitionSpec as P


D = 8192
EPS = 1e-05
NX, NY, NZ, NW, NC = 4, 2, 8, 2, 2
AXES = ("x", "y", "z", "w", "c")
PROMPT = ("x", "y")
TENSOR = ("z", "w", "c")
BF, F32 = jnp.bfloat16, jnp.float32


def shifted(array, axis, size, step):
    return lax.ppermute(array, axis, [(i, (i + step) % size) for i in range(size)])


def paired(array, axis, size, bit):
    return lax.ppermute(array, axis, [(i, i ^ bit) for i in range(size)])


def wide(array):
    return array.astype(F32)


def paired_prompt(array, k):
    return lax.ppermute(array, PROMPT, [(p, p ^ k) for p in range(NX * NY)])


def blocks_kernel(tokens_ref, *out_refs):
    place = lax.axis_index("x") * NY + lax.axis_index("y")
    half, share = out_refs[0].shape
    first = pl.multiple_of(lax.axis_index("c") * half, half)
    for k, out_ref in enumerate(out_refs):
        start = pl.multiple_of((place ^ k) * share, share)
        out_ref[...] = tokens_ref[pl.ds(first, half), pl.ds(start, share)]


def tokens_for_block(tokens):
    count = NX * NY
    block = jax.ShapeDtypeStruct((tokens.shape[0] // NC, D // count), tokens.dtype)
    own = pl.pallas_call(blocks_kernel, out_shape=[block] * count)(tokens)
    own = list(own)
    for k in (4, 5, 2, 3, 6, 7, 1):
        own[k] = paired_prompt(own[k], k)
    own = jnp.stack(own)
    other = paired(own, "c", NC, 1)
    return [rows.reshape(NX, NY, *block.shape) for rows in (own, other)]


def at(array, index, axis):
    return lax.dynamic_index_in_dim(array, index, axis, keepdims=False)


def products(rows, weights):
    flat = rows.reshape(-1, rows.shape[-1])
    outs = [jnp.dot(flat, weight, preferred_element_type=F32) for weight in weights]
    return [out.reshape(*rows.shape[:-1], -1) for out in outs]


def joined(pair):
    return jnp.stack([part.astype(BF) for part in pair])


def step(tokens, gate_weight, up_weight, down_weight, norm_gain, unembed, guidance, logit_bias):
    x, y, z, _, c = (lax.axis_index(axis) for axis in AXES)
    tokens = tokens[0]
    own, other = tokens_for_block(tokens)
    both = (gate_weight, up_weight)

    pb = products(own, both)
    swap_b = paired(joined([p[:, 1] for p in pb]), "y", NY, 1)
    pa = products(other, both)
    packed_a = [joined([p[d] for p in pa]) for d in TURNS]
    got_a = [paired(packed, "x", NX, d) for d, packed in zip(TURNS, packed_a)]
    sum_a = [p[0] + sum(wide(got[i]) for got in got_a) for i, p in enumerate(pa)]
    swap_a = paired(joined([p[1] for p in sum_a]), "y", NY, 1)
    sum_b = [p[:, 0] + wide(got) for p, got in zip(pb, swap_b)]
    got_b = [paired(joined([p[d] for p in sum_b]), "x", NX, d) for d in TURNS]
    gate_a, up_a = [p[0] + wide(got) for p, got in zip(sum_a, swap_a)]
    hidden_a = (jax.nn.silu(gate_a) * up_a).astype(BF)
    gate_b, up_b = [p[0] + sum(wide(got[i]) for got in got_b) for i, p in enumerate(sum_b)]
    hidden_b = (jax.nn.silu(gate_b) * up_b).astype(BF)

    line_a = [hidden_a] + [None] * (NX - 1)
    for d in TURNS:
        line_a[d] = paired(hidden_a, "x", NX, d)
    line_a = jnp.stack(line_a)
    all_a = jnp.stack([line_a, paired(line_a, "y", NY, 1)], axis=1)
    pair_b = jnp.stack([hidden_b, paired(hidden_b, "y", NY, 1)])
    all_b = [pair_b] + [None] * (NX - 1)
    for d in TURNS:
        all_b[d] = paired(pair_b, "x", NX, d)
    all_b = jnp.stack(all_b)

    (down_a,) = products(all_a, (down_weight,))
    passed = paired(down_a.astype(BF), "c", NC, 1)
    (down_b,) = products(all_b, (down_weight,))
    part = (down_b + wide(passed)).astype(BF)
    share = part.shape[-1]
    part = part.reshape(NX * NY, NZ, -1, share)

    def piece(k):
        return lax.dynamic_index_in_dim(part, (z + k) % NZ, 1, keepdims=False)

    def sent(block, step):
        return shifted(block, "z", NZ, step)

    cut = NX * NY // 2
    far = piece(4)
    far_up, far_down = sent(far[:cut], 2), sent(far[cut:], -2)
    relay_up, relay_down = sent(piece(3), 1), sent(piece(5), -1)
    two_up = wide(piece(2)) + wide(relay_up)
    two_up = jnp.concatenate([two_up[:cut] + wide(far_up), two_up[cut:]]).astype(BF)
    two_down = wide(piece(6)) + wide(relay_down)
    two_down = jnp.concatenate([two_down[:cut], two_down[cut:] + wide(far_down)]).astype(BF)
    two_up, two_down = sent(two_up, 2), sent(two_down, -2)
    one_up, one_down = sent(piece(1), 1), sent(piece(7), -1)
    mine = wide(piece(0)) + sum(wide(got) for got in (one_up, one_down, two_up, two_down))
    mine = mine.astype(BF)
    branch = wide(mine) + wide(shifted(mine, "w", NW, 1))

    residual = at(own.reshape(NX * NY, NZ, -1, share), z, 1)
    state = wide(residual) + branch
    partial_square = jnp.sum(state * state, axis=2)
    offsets = jnp.arange(NX * NY)
    variant_at = offsets ^ (x * NY + y)
    placed_at = (variant_at[None, :] == offsets[:, None]).astype(F32)
    by_variant = jnp.sum(placed_at[:, :, None] * partial_square[None], axis=1)
    everyone = lax.all_to_all(
        jnp.broadcast_to(by_variant[None], (NX * NY, *by_variant.shape)),
        PROMPT, 0, 0, tiled=True,
    )
    square = everyone.sum(axis=0)
    scale = lax.rsqrt(square / D + EPS) * guidance[:, None]
    scale = jnp.sum(placed_at[:, :, None] * scale[:, None], axis=0)
    mixed = (jnp.sum(state * scale[:, :, None], axis=0) * norm_gain).astype(BF)

    ring = jnp.broadcast_to(mixed[None], (NZ, *mixed.shape))
    ring = lax.all_to_all(ring, "z", 0, 0, tiled=True).reshape(-1, share)
    peer = paired(ring, "c", NC, 1)
    first = jnp.where(c == 0, ring, peer)
    second = jnp.where(c == 0, peer, ring)
    rows = jnp.concatenate([first, second])

    product = jnp.dot(rows, unembed, preferred_element_type=F32).astype(BF)
    tiles = product.reshape(NX * NY, -1, product.shape[-1])
    tiles = lax.all_to_all(tiles, PROMPT, 0, 0, tiled=True)
    scores = jnp.sum(wide(tiles), axis=0) + logit_bias
    top = jnp.max(scores, axis=1, keepdims=True)
    part_lse = top[:, 0] + jnp.log(jnp.sum(jnp.exp(scores - top), axis=1))
    shards = NZ * NW * NC
    part_lse = lax.all_to_all(
        jnp.broadcast_to(part_lse[None, None], (shards, 1, part_lse.shape[0])),
        TENSOR, 0, 0, tiled=True,
    )
    lse = jax.nn.logsumexp(part_lse[:, 0], axis=0)
    return scores - lse[:, None]


TURNS = (2, 1, 3)
TURNS = (2, 1, 3)


def solution(mesh):
    finer = Mesh(mesh.devices.reshape(NX, NY, NZ, NW, NC), AXES)
    placed = (
        P(PROMPT, None, None),
        P(PROMPT, TENSOR),
        P(PROMPT, TENSOR),
        P(TENSOR, PROMPT),
        P(PROMPT),
        P(PROMPT, TENSOR),
        P(),
        P(PROMPT, TENSOR),
    )
    return jax.shard_map(
        step, mesh=finer, in_specs=placed, out_specs=P(PROMPT, TENSOR), check_vma=False
    )
```
